32 devices in a mesh: row: 8 (over z, x), col: 4 (over y, core).
Axes of the slice: x: 2, y: 2, z: 4, core: 2. Of those that a mesh axis runs over, the one named last changes fastest.
Arguments:
- mel: float32 [128, 18432], P('col', 'row'), may hold values from -6 to 6
- pair_val: int32 [128], replicated, may hold values from 0 to 31
- pair_cond: int32 [128], replicated, may hold values from 0 to 31
- val_energy: float32 [32], replicated, may hold values from -8 to -1
- cond_energy: float32 [32], replicated, may hold values from 1 to 8
- freqs: float32 [2], replicated, may hold values from 0.5 to 6
Outputs:
- chi: float32 [2, 18432, 18432], P(None, 'row', 'col')
The draws below stay inside these ranges and needn't reach their ends.
All inputs are finite; a program needn't handle non-finite values.
Results may differ from the reference program's by a relative error of at most 0.000098.
Values sent between devices are 32-bit elements; how exact they have to be, the bound alone decides.
A program may use at most 128 MiB of HBM per device.

```python
import math
import jax
import jax.numpy as jnp
from jax import lax

NG = 18432
PAIRS = 128
NV = 32
NC = 32
NFREQ = 2


def place_ends(drawn, own_key, low, top_value):
    spot = [jax.random.randint(jax.random.fold_in(own_key, axis), (), 0, length) for axis, length in enumerate(drawn.shape)]
    widest = drawn.shape.index(max(drawn.shape))
    next_to = spot[:widest] + [(spot[widest] + 1) % drawn.shape[widest]] + spot[widest + 1:]
    return drawn.at[tuple(spot)].set(low).at[tuple(next_to)].set(top_value)


def shard_levels(stream_key, extent, cuts, low, largest):
    factor_of, own = 1.0, jax.random.fold_in(stream_key, 6)
    for position, blocks in cuts:
        heights = jnp.exp(jax.random.uniform(jax.random.fold_in(own, position), (blocks,), jnp.float32, low / len(cuts), largest / len(cuts)))
        factor_of = factor_of * jnp.repeat(heights, extent[position] // blocks).reshape([-1 if axis == position else 1 for axis in range(len(extent))])
    return factor_of


def centred(own_key, dims, width, bound, cuts=(), dtype=jnp.bfloat16):
    entries = jax.random.normal(own_key, dims, jnp.float32) * width
    if len(cuts) > 0:
        entries = shard_levels(own_key, dims, cuts, -0.22, 0.18) * entries
    return jnp.clip(entries, min=-bound, max=bound).astype(dtype)


def setup_inputs(seed: int = 0) -> dict:
    streams_of = jax.random.split(jax.random.key(seed), 7)
    return {
        "mel": centred(streams_of[0], (PAIRS, NG), 1.0, 6.0, ((0, 4), (1, 8)), jnp.float32),
        "pair_val": place_ends(jax.random.randint(streams_of[1], (PAIRS,), 0, NV), jax.random.fold_in(streams_of[1], 1), 0, NV - 1).astype(jnp.int32),
        "pair_cond": place_ends(jax.random.randint(streams_of[2], (PAIRS,), 0, NC), jax.random.fold_in(streams_of[2], 1), 0, NC - 1).astype(jnp.int32),
        "val_energy": jnp.clip(jax.random.uniform(streams_of[3], (NV,), jnp.float32, -8.0, -1.0), -8.0, -1.0),
        "cond_energy": jnp.clip(jax.random.uniform(streams_of[4], (NC,), jnp.float32, 1.0, 8.0), 1.0, 8.0),
        "freqs": jnp.clip(jax.random.uniform(streams_of[5], (NFREQ,), jnp.float32, 0.5, 6.0), 0.5, 6.0),
    }


def reference(mel, pair_val, pair_cond, val_energy, cond_energy, freqs):
    gap = cond_energy[pair_cond] - val_energy[pair_val]
    scale = 1.0 / math.sqrt(PAIRS)
    weights = -4.0 * gap[None, :] / (gap[None, :] * gap[None, :] + freqs[:, None] * freqs[:, None]) * scale

    def one_freq(weight_row):
        scaled = mel * weight_row[:, None]
        return lax.dot_general(scaled, mel, (((0,), (0,)), ((), ())), precision=lax.Precision.HIGHEST, preferred_element_type=jnp.float32)
    return lax.map(one_freq, weights)
```

```python
import functools
import math

import jax
import jax.numpy as jnp
from jax import lax
from jax.experimental import pallas as pl
from jax.experimental.pallas import tpu as pltpu
from jax.sharding import PartitionSpec as P

PAIRS = 128
MESH = pl.DeviceIdType.MESH
PIECES = 3


def pair_weights(pair_val, pair_cond, val_energy, cond_energy, freqs):
    cond_onehot = (
        pair_cond[:, None] == jnp.arange(cond_energy.shape[0], dtype=jnp.int32)[None, :]
    ).astype(jnp.float32)
    val_onehot = (
        pair_val[:, None] == jnp.arange(val_energy.shape[0], dtype=jnp.int32)[None, :]
    ).astype(jnp.float32)
    gap = jnp.sum(cond_onehot * cond_energy[None, :], axis=1) - jnp.sum(
        val_onehot * val_energy[None, :], axis=1
    )
    scale = 1.0 / math.sqrt(PAIRS)
    return (
        -4.0
        * gap[:, None]
        / (gap[:, None] * gap[:, None] + freqs[None, :] * freqs[None, :])
        * scale
    )


def split(x):
    hi = x.astype(jnp.bfloat16)
    return hi, (x - hi.astype(jnp.float32)).astype(jnp.bfloat16)


def gather_kernel(
    span, w_ref, mel_ref, lhs_ref, rhs_ref, rows, own, other,
    load_sem, row_send, row_recv, up_send, down_send, own_recv, swap_send, swap_recv,
):
    r, c = lax.axis_index("row"), lax.axis_index("col")
    group, place = r // span, r % span
    depth, width = mel_ref.shape
    groups = 4
    pairs = groups * depth
    core = c + 1 - 2 * (c % 2)
    chip = c + 2 - 4 * (c // 2)
    both = core + 2 - 4 * (core // 2)
    beside = r + 1 - 2 * place
    up, down = r + span, r - span
    has_up, has_down = group < groups - 1, group > 0
    source = group == c
    send_up = (group >= c) & has_up
    send_down = (group <= c) & has_down

    load = pltpu.make_async_copy(mel_ref, rows.at[0], load_sem)
    load.start()
    barrier = pltpu.get_barrier_semaphore()
    for device in ((r, core), (r, chip), (beside, c)):
        pl.semaphore_signal(barrier, inc=1, device_id=device, device_id_type=MESH)

    @pl.when(has_up)
    def _():
        pl.semaphore_signal(barrier, inc=1, device_id=(up, c), device_id_type=MESH)

    @pl.when(has_down)
    def _():
        pl.semaphore_signal(barrier, inc=1, device_id=(down, c), device_id_type=MESH)

    pl.semaphore_wait(barrier, 3 + has_up.astype(jnp.int32) + has_down.astype(jnp.int32))
    load.wait()

    step = width // PIECES

    def view(ref, t, p):
        return ref.at[t, :, pl.ds(p * step, step)]

    def send(src, s, dst, t, p, send_sem, recv_sem, device):
        return pltpu.make_async_remote_copy(
            src_ref=view(src, s, p), dst_ref=view(dst, t, p), send_sem=send_sem, recv_sem=recv_sem,
            device_id=device, device_id_type=MESH,
        )

    def row_copy(t, p):
        device = (r, chip) if t == 2 else (r, core)
        return send(rows, 2 if t == 3 else 0, rows, t, p, row_send.at[t - 1, p], row_recv.at[t - 1, p], device)

    def up_copy(src, t, p):
        return send(src, t, own, t, p, up_send.at[t, p], own_recv.at[t, p], (up, c))

    def down_copy(src, t, p):
        return send(src, t, own, t, p, down_send.at[t, p], own_recv.at[t, p], (down, c))

    def swap_copy(src, t, p):
        return send(src, t, other, t, p, swap_send.at[t, p], swap_recv.at[t, p], (beside, c))

    def put_rhs(src, t, p, offset):
        hi, lo = split(src[t, :, pl.ds(p * step, step)])
        at = pl.ds(pl.multiple_of(offset + p * step, 128), step)
        rhs_ref[pl.ds(t * depth, depth), at] = hi
        rhs_ref[pl.ds(pairs + t * depth, depth), at] = lo

    for p in range(PIECES):
        row_copy(1, p).start()
        row_copy(2, p).start()
    for t in range(groups):
        for p in range(PIECES):
            if t > 0:
                row_copy(t, p).wait_recv()
            if t == 2:
                row_copy(3, p).start()

            @pl.when(source)
            def _():
                swap_copy(rows, t, p).start()

                @pl.when(has_up)
                def _():
                    up_copy(rows, t, p).start()

                @pl.when(has_down)
                def _():
                    down_copy(rows, t, p).start()

                put_rhs(rows, t, p, place * width)

            @pl.when(jnp.logical_not(source))
            def _():
                up_copy(own, t, p).wait_recv()
                swap_copy(own, t, p).start()

                @pl.when(send_up)
                def _():
                    up_copy(own, t, p).start()

                @pl.when(send_down)
                def _():
                    down_copy(own, t, p).start()

                put_rhs(own, t, p, place * width)

            if t == groups - 1:
                w = jnp.concatenate(
                    [w_ref[pl.ds(pl.multiple_of(q * depth, depth), depth), :] for q in (c, core, chip, both)], axis=0
                )
                block = rows[:, :, pl.ds(p * step, step)].reshape(pairs, step)
                for f in range(w.shape[1]):
                    hi, lo = split((block * w[:, f:f + 1]).T)
                    at = pl.ds(p * step, step)
                    lhs_ref[f, at, 0:pairs] = hi
                    lhs_ref[f, at, pairs:2 * pairs] = hi
                    lhs_ref[f, at, 2 * pairs:] = lo
    for t in range(groups):
        for p in range(PIECES):
            swap_copy(own, t, p).wait_recv()
            put_rhs(other, t, p, (1 - place) * width)
    for t in range(groups):
        for p in range(PIECES):
            if t > 0:
                row_copy(t, p).wait_send()
            swap_copy(own, t, p).wait_send()

            @pl.when(send_up)
            def _():
                up_copy(own, t, p).wait_send()

            @pl.when(send_down)
            def _():
                down_copy(own, t, p).wait_send()


def gather(mel, weights, span):
    depth, width = mel.shape
    nf = weights.shape[1]
    dma = pltpu.SemaphoreType.DMA
    return pl.pallas_call(
        functools.partial(gather_kernel, span),
        out_shape=(
            jax.ShapeDtypeStruct((nf, width, 12 * depth), jnp.bfloat16),
            jax.ShapeDtypeStruct((8 * depth, span * width), jnp.bfloat16),
        ),
        in_specs=[pl.BlockSpec(memory_space=pltpu.VMEM), pl.BlockSpec(memory_space=pl.ANY)],
        out_specs=(pl.BlockSpec(memory_space=pltpu.VMEM), pl.BlockSpec(memory_space=pltpu.VMEM)),
        scratch_shapes=[pltpu.VMEM((4, depth, width), jnp.float32)] * 3
        + [dma, dma((3, PIECES)), dma((3, PIECES))]
        + [dma((4, PIECES))] * 5,
        compiler_params=pltpu.CompilerParams(
            collective_id=0, has_side_effects=True, vmem_limit_bytes=48 * 1024 * 1024
        ),
    )(weights, mel)


def product_kernel(lhs_ref, rhs_ref, out_ref):
    pairs = rhs_ref.shape[0] // 2
    rhs = rhs_ref[...]
    for f in range(out_ref.shape[0]):
        out_ref[f] = jnp.dot(
            lhs_ref[f], jnp.concatenate([rhs, rhs[:pairs]], axis=0), preferred_element_type=jnp.float32
        )


def product(lhs, rhs, tile=512):
    nf, height, depth = lhs.shape
    columns = rhs.shape[1]
    return pl.pallas_call(
        product_kernel,
        grid=(columns // tile,),
        out_shape=jax.ShapeDtypeStruct((nf, height, columns), jnp.float32),
        in_specs=[
            pl.BlockSpec((nf, height, depth), lambda i: (0, 0, 0), pipeline_mode=pl.Buffered(1)),
            pl.BlockSpec((rhs.shape[0], tile), lambda i: (0, i)),
        ],
        out_specs=pl.BlockSpec((nf, height, tile), lambda i: (0, 0, i)),
        compiler_params=pltpu.CompilerParams(vmem_limit_bytes=56 * 1024 * 1024),
    )(lhs, rhs)


def body(rows, cols, mel, pair_val, pair_cond, val_energy, cond_energy, freqs):
    weights = pair_weights(pair_val, pair_cond, val_energy, cond_energy, freqs)
    if cols == 4 and rows == 8 and mel.shape[0] % 16 == 0 and mel.shape[1] % (128 * PIECES) == 0:
        return product(*gather(mel, weights, rows // cols))
    rows_all = lax.all_gather(mel, "col", axis=0, tiled=True)
    own_block = lax.all_gather(mel, "row", axis=1, tiled=True)
    col_block = lax.all_to_all(own_block, "col", split_axis=1, concat_axis=0, tiled=True)
    scaled = weights.T[:, :, None] * rows_all[None, :, :]
    return lax.dot_general(
        scaled,
        col_block,
        (((1,), (0,)), ((), ())),
        precision=lax.Precision.HIGHEST,
        preferred_element_type=jnp.float32,
    )


def solution(mesh):
    return jax.shard_map(
        functools.partial(body, mesh.shape["row"], mesh.shape["col"]),
        mesh=mesh,
        in_specs=(P("col", "row"), P(), P(), P(), P(), P()),
        out_specs=P(None, "row", "col"),
        check_vma=False,
    )
```

```python
import functools
import math

import jax
import jax.numpy as jnp
from jax import lax
from jax.experimental import pallas as pl
from jax.experimental.pallas import tpu as pltpu
from jax.sharding import PartitionSpec as P

PAIRS = 128
MESH = pl.DeviceIdType.MESH
PIECES = 6
SWAPPED = 2
ALTERNATE = ((3,), (2, 3))
MIB = 1024 * 1024


def pair_weights(pair_val, pair_cond, val_energy, cond_energy, freqs):
    cond_onehot = (
        pair_cond[:, None] == jnp.arange(cond_energy.shape[0], dtype=jnp.int32)[None, :]
    ).astype(jnp.float32)
    val_onehot = (
        pair_val[:, None] == jnp.arange(val_energy.shape[0], dtype=jnp.int32)[None, :]
    ).astype(jnp.float32)
    gap = jnp.sum(cond_onehot * cond_energy[None, :], axis=1) - jnp.sum(
        val_onehot * val_energy[None, :], axis=1
    )
    scale = 1.0 / math.sqrt(PAIRS)
    return (
        -4.0
        * gap[None, :]
        / (gap[None, :] * gap[None, :] + freqs[:, None] * freqs[:, None])
        * scale
    )


def split(x):
    hi = x.astype(jnp.bfloat16)
    return hi, (x - hi.astype(jnp.float32)).astype(jnp.bfloat16)


def picked(energy, index):
    n = energy.shape[1]
    square = (n, n)
    eye = lax.broadcasted_iota(jnp.int32, square, 0) == lax.broadcasted_iota(jnp.int32, square, 1)
    column = jnp.sum(jnp.where(eye, energy, 0.0), axis=1, keepdims=True)
    onehot = lax.broadcasted_iota(jnp.int32, (n, index.shape[1]), 0) == index
    return jnp.sum(jnp.where(onehot, column, 0.0), axis=0, keepdims=True)


def gather_kernel(
    span, pv_ref, pc_ref, ve_ref, ce_ref, fr_ref, mel_ref, lhs_ref, rhs_ref, tail_ref, rows, own, other, alt,
    load_sem, row_send, row_recv, up_send, down_send, own_recv, swap_send, swap_recv,
    alt_up_send, alt_down_send, alt_recv, cross_send,
):
    r, c = lax.axis_index("row"), lax.axis_index("col")
    group, place = r // span, r % span
    depth, width = mel_ref.shape
    groups = 4
    pairs = groups * depth
    step = width // PIECES
    core = c + 1 - 2 * (c % 2)
    chip = c + 2 - 4 * (c // 2)
    both = core + 2 - 4 * (core // 2)
    order = (c, core, chip, both)
    alt_order = (chip, both, c, core)
    beside = r + 1 - 2 * place
    up, down = r + span, r - span
    has_up, has_down = group < groups - 1, group > 0
    source, alt_source = group == c, group == chip
    send_up, send_down = (group >= c) & has_up, (group <= c) & has_down
    alt_send_up, alt_send_down = (group >= chip) & has_up, (group <= chip) & has_down

    load = pltpu.make_async_copy(mel_ref, rows.at[c], load_sem)
    load.start()
    barrier = pltpu.get_barrier_semaphore()
    for device in ((r, core), (r, chip), (beside, c)):
        pl.semaphore_signal(barrier, inc=1, device_id=device, device_id_type=MESH)

    @pl.when(has_up)
    def _():
        pl.semaphore_signal(barrier, inc=1, device_id=(up, c), device_id_type=MESH)

    @pl.when(has_down)
    def _():
        pl.semaphore_signal(barrier, inc=1, device_id=(down, c), device_id_type=MESH)

    pl.semaphore_wait(barrier, 3 + has_up.astype(jnp.int32) + has_down.astype(jnp.int32))
    load.wait()

    def columns(p, offset=0):
        start = offset + p * step
        return pl.ds(start if isinstance(start, int) else pl.multiple_of(start, 128), step)

    def send(src, dst, q, p, send_sem, recv_sem, device):
        return pltpu.make_async_remote_copy(
            src_ref=src.at[q, :, columns(p)], dst_ref=dst.at[q, :, columns(p)], send_sem=send_sem, recv_sem=recv_sem,
            device_id=device, device_id_type=MESH,
        )

    def row_copy(t, p):
        device = (r, chip) if t == 2 else (r, core)
        return send(rows, rows, chip if t == 3 else c, p, row_send.at[t - 1, p], row_recv.at[t - 1, p], device)

    def up_copy(src, t, p):
        return send(src, own, order[t], p, up_send.at[t, p], own_recv.at[t, p], (up, c))

    def down_copy(src, t, p):
        return send(src, own, order[t], p, down_send.at[t, p], own_recv.at[t, p], (down, c))

    def swap_copy(src, t, p):
        return send(src, other, order[t], p, swap_send.at[t, p], swap_recv.at[t, p], (beside, c))

    def alt_up_copy(src, t, p):
        return send(src, alt, alt_order[t], p, alt_up_send.at[t - 2, p], alt_recv.at[t - 2, p], (up, c))

    def alt_down_copy(src, t, p):
        return send(src, alt, alt_order[t], p, alt_down_send.at[t - 2, p], alt_recv.at[t - 2, p], (down, c))

    def cross_copy(src, t, p):
        return send(src, own, alt_order[t], p, cross_send.at[t - 2, p], own_recv.at[t, p], (r, chip))

    def put_rhs(src, q, p, offset):
        hi, lo = split(src[q, :, columns(p)])
        at = columns(p, offset)
        first = pl.multiple_of(q * depth, depth)
        rhs_ref[pl.ds(first, depth), at] = hi
        rhs_ref[pl.ds(pl.multiple_of(pairs + q * depth, depth), depth), at] = lo

    def finish(src, t, p):
        if p < SWAPPED:
            swap_copy(src, t, p).start()
        else:
            first = pl.multiple_of(order[t] * depth, depth)
            tail_ref[pl.ds(first, depth), columns(p - SWAPPED)] = src[order[t], :, columns(p)]
        put_rhs(src, order[t], p, place * width)

    for p in range(PIECES):
        row_copy(2, p).start()
        row_copy(1, p).start()

    gap = picked(ce_ref[...], pc_ref[...]) - picked(ve_ref[...], pv_ref[...])
    scale = 1.0 / math.sqrt(PAIRS)
    weights = []
    for f in range(fr_ref.shape[1]):
        freq = fr_ref[:, f:f + 1]
        weights.append(-4.0 * gap / (gap * gap + freq * freq) * scale)

    for p in range(PIECES):
        away = ALTERNATE[p % len(ALTERNATE)]
        row_copy(1, p).wait_recv()
        for t in away:
            @pl.when(alt_source)
            def _():
                @pl.when(has_up)
                def _():
                    alt_up_copy(rows, t, p).start()

                @pl.when(has_down)
                def _():
                    alt_down_copy(rows, t, p).start()

        for t in range(groups):
            if t >= 2:
                row_copy(t, p).wait_recv()
            if t == 2:
                row_copy(3, p).start()

            @pl.when(source)
            def _():
                if t not in away:
                    @pl.when(has_up)
                    def _():
                        up_copy(rows, t, p).start()

                    @pl.when(has_down)
                    def _():
                        down_copy(rows, t, p).start()

                finish(rows, t, p)

            if t not in away:
                @pl.when(jnp.logical_not(source))
                def _():
                    up_copy(own, t, p).wait_recv()

                    @pl.when(send_up)
                    def _():
                        up_copy(own, t, p).start()

                    @pl.when(send_down)
                    def _():
                        down_copy(own, t, p).start()

                    finish(own, t, p)

        for t in away:
            @pl.when(jnp.logical_not(alt_source))
            def _():
                alt_up_copy(alt, t, p).wait_recv()

                @pl.when(alt_send_up)
                def _():
                    alt_up_copy(alt, t, p).start()

                @pl.when(alt_send_down)
                def _():
                    alt_down_copy(alt, t, p).start()

                cross_copy(alt, t, p).start()

        for t in ALTERNATE[(p - 1) % len(ALTERNATE)] if p > 0 else ():
            @pl.when(jnp.logical_not(source))
            def _():
                up_copy(own, t, p - 1).wait_recv()
                finish(own, t, p - 1)

        block = rows[:, :, columns(p)].reshape(pairs, step).T
        for f in range(fr_ref.shape[1]):
            hi, lo = split(block * weights[f])
            lhs_ref[f, columns(p), 0:pairs] = hi
            lhs_ref[f, columns(p), pairs:2 * pairs] = lo

    for t in ALTERNATE[(PIECES - 1) % len(ALTERNATE)]:
        @pl.when(jnp.logical_not(source))
        def _():
            up_copy(own, t, PIECES - 1).wait_recv()
            finish(own, t, PIECES - 1)

    for p in range(SWAPPED):
        for t in range(groups):
            swap_copy(own, t, p).wait_recv()
            put_rhs(other, order[t], p, (1 - place) * width)
    for p in range(PIECES):
        away = ALTERNATE[p % len(ALTERNATE)]
        for t in range(groups):
            if t > 0:
                row_copy(t, p).wait_send()
            if p < SWAPPED:
                swap_copy(own, t, p).wait_send()
            if t in away:
                @pl.when(alt_send_up)
                def _():
                    alt_up_copy(alt, t, p).wait_send()

                @pl.when(alt_send_down)
                def _():
                    alt_down_copy(alt, t, p).wait_send()

                @pl.when(jnp.logical_not(alt_source))
                def _():
                    cross_copy(alt, t, p).wait_send()
            else:
                @pl.when(send_up)
                def _():
                    up_copy(own, t, p).wait_send()

                @pl.when(send_down)
                def _():
                    down_copy(own, t, p).wait_send()


def gather(mel, small, span):
    depth, width = mel.shape
    nf = small[-1].shape[1]
    dma = pltpu.SemaphoreType.DMA
    four, two = dma((4, PIECES)), dma((2, PIECES))
    vmem = pl.BlockSpec(memory_space=pltpu.VMEM)
    return pl.pallas_call(
        functools.partial(gather_kernel, span),
        out_shape=(
            jax.ShapeDtypeStruct((nf, width, 8 * depth), jnp.bfloat16),
            jax.ShapeDtypeStruct((8 * depth, span * width), jnp.bfloat16),
            jax.ShapeDtypeStruct((4 * depth, width - SWAPPED * (width // PIECES)), jnp.float32),
        ),
        in_specs=[vmem] * 5 + [pl.BlockSpec(memory_space=pltpu.HBM)],
        out_specs=(vmem, vmem, vmem),
        scratch_shapes=[pltpu.VMEM((4, depth, width), jnp.float32)] * 4
        + [dma, dma((3, PIECES)), dma((3, PIECES))]
        + [four] * 5 + [two] * 4,
        compiler_params=pltpu.CompilerParams(
            collective_id=0, has_side_effects=True, vmem_limit_bytes=20 * MIB
        ),
    )(*small, mel)


def multiply(lhs_ref, rhs_hi, rhs_lo, out_ref):
    height = out_ref.shape[1]
    pairs = rhs_hi.shape[0]
    at = pl.ds(pl.multiple_of(pl.program_id(1) * height, height), height)
    right = jnp.concatenate([rhs_hi, rhs_hi, rhs_lo], axis=0)
    for f in range(out_ref.shape[0]):
        left = lhs_ref[f, at, :]
        out_ref[f] = jnp.dot(
            jnp.concatenate([left, left[:, :pairs]], axis=1), right, preferred_element_type=jnp.float32
        )


def first_kernel(place_ref, lhs_ref, rhs_ref, out_ref):
    pairs = rhs_ref.shape[0] // 2
    tile = out_ref.shape[2]
    count = rhs_ref.shape[1] // tile
    index = (pl.program_id(0) + place_ref[0] * (count // 2)) % count
    at = pl.ds(pl.multiple_of(index * tile, tile), tile)
    multiply(lhs_ref, rhs_ref[:pairs, at], rhs_ref[pairs:, at], out_ref)


def second_kernel(place_ref, lhs_ref, tail_ref, done_ref, out_ref):
    tile = out_ref.shape[2]
    at = pl.ds(pl.multiple_of(pl.program_id(0) * tile, tile), tile)
    hi, lo = split(tail_ref[:, at])
    multiply(lhs_ref, hi, lo, out_ref)


def product(lhs, rhs, tail, place, tail_of):
    nf, width, _ = lhs.shape
    columns = rhs.shape[1]
    tile = width // 3
    height = width // 2
    count = columns // tile
    last = tail.shape[1] // tile
    out = jax.ShapeDtypeStruct((nf, width, columns), jnp.float32)
    vmem = pl.BlockSpec(memory_space=pltpu.VMEM)

    def call(kernel, start, steps, operands, specs, aliases):
        flops = 2 * 3 * nf * width * PAIRS * tile * steps
        return pl.pallas_call(
            kernel,
            out_shape=out,
            grid_spec=pltpu.PrefetchScalarGridSpec(
                num_scalar_prefetch=1,
                grid=(steps, width // height),
                in_specs=specs,
                out_specs=pl.BlockSpec(
                    (nf, height, tile), lambda i, m, at: (0, m, (i + start + at[0] * (count // 2)) % count)
                ),
            ),
            input_output_aliases=aliases,
            cost_estimate=pl.CostEstimate(
                flops=flops, bytes_accessed=nf * width * tile * steps * 4, transcendentals=0
            ),
            compiler_params=pltpu.CompilerParams(vmem_limit_bytes=32 * MIB),
        )(place, *operands)

    done = call(first_kernel, 0, count - last, (lhs, rhs), [vmem, vmem], {})
    return call(
        second_kernel, count - last, last, (lhs, tail_of(tail), done), [vmem, vmem, pl.BlockSpec(memory_space=pl.ANY)], {3: 0}
    )


def body(rows, cols, mel, pair_val, pair_cond, val_energy, cond_energy, freqs):
    if cols == 4 and rows == 8 and mel.shape[0] % 16 == 0 and mel.shape[1] % (128 * PIECES) == 0:
        span = rows // cols
        small = [x[None, :] for x in (pair_val, pair_cond, val_energy, cond_energy, freqs)]
        place = (lax.axis_index("row") % span).astype(jnp.int32)[None]
        pairs = [(r, r + 1 - 2 * (r % span)) for r in range(rows)]
        return product(*gather(mel, small, span), place, lambda tail: lax.ppermute(tail, "row", pairs))
    weights = pair_weights(pair_val, pair_cond, val_energy, cond_energy, freqs)
    rows_all = lax.all_gather(mel, "col", axis=0, tiled=True)
    own_block = lax.all_gather(mel, "row", axis=1, tiled=True)
    col_block = lax.all_to_all(own_block, "col", split_axis=1, concat_axis=0, tiled=True)
    scaled = weights[:, :, None] * rows_all[None, :, :]
    return lax.dot_general(
        scaled,
        col_block,
        (((1,), (0,)), ((), ())),
        precision=lax.Precision.HIGHEST,
        preferred_element_type=jnp.float32,
    )


def solution(mesh):
    return jax.shard_map(
        functools.partial(body, mesh.shape["row"], mesh.shape["col"]),
        mesh=mesh,
        in_specs=(P("col", "row"), P(), P(), P(), P(), P()),
        out_specs=P(None, "row", "col"),
        check_vma=False,
    )
```

```python
import functools
import math

import jax
import jax.numpy as jnp
from jax import lax
from jax.experimental import pallas as pl
from jax.experimental.pallas import tpu as pltpu
from jax.sharding import PartitionSpec as P

PAIRS = 128
MESH = pl.DeviceIdType.MESH
PIECES = 6
SWAPPED = 2
LEAD = 3
CROSS_LAG = 2
ALTERNATE = ((3,), (2, 3))
MIB = 1024 * 1024


def pair_weights(pair_val, pair_cond, val_energy, cond_energy, freqs):
    cond_onehot = (
        pair_cond[:, None] == jnp.arange(cond_energy.shape[0], dtype=jnp.int32)[None, :]
    ).astype(jnp.float32)
    val_onehot = (
        pair_val[:, None] == jnp.arange(val_energy.shape[0], dtype=jnp.int32)[None, :]
    ).astype(jnp.float32)
    gap = jnp.sum(cond_onehot * cond_energy[None, :], axis=1) - jnp.sum(
        val_onehot * val_energy[None, :], axis=1
    )
    scale = 1.0 / math.sqrt(PAIRS)
    return (
        -4.0
        * gap[None, :]
        / (gap[None, :] * gap[None, :] + freqs[:, None] * freqs[:, None])
        * scale
    )


def split(x):
    hi = x.astype(jnp.bfloat16)
    return hi, (x - hi.astype(jnp.float32)).astype(jnp.bfloat16)


def gather_kernel(
    span, w_ref, mel_ref, lhs_ref, rhs_ref, tail_ref, rows, own, other, alt,
    load_sem, row_send, row_recv, up_send, down_send, own_recv, swap_send, swap_recv,
    alt_up_send, alt_down_send, alt_recv, cross_send,
):
    r, c = lax.axis_index("row"), lax.axis_index("col")
    group, place = r // span, r % span
    depth, width = mel_ref.shape
    groups = 4
    pairs = groups * depth
    step = width // PIECES
    core = c + 1 - 2 * (c % 2)
    chip = c + 2 - 4 * (c // 2)
    both = core + 2 - 4 * (core // 2)
    order = (c, core, chip, both)
    alt_order = (chip, both, c, core)
    beside = r + 1 - 2 * place
    up, down = r + span, r - span
    has_up, has_down = group < groups - 1, group > 0
    source, alt_source = group == c, group == chip
    send_up, send_down = (group >= c) & has_up, (group <= c) & has_down
    alt_send_up, alt_send_down = (group >= chip) & has_up, (group <= chip) & has_down

    load = pltpu.make_async_copy(mel_ref, rows.at[c], load_sem)
    load.start()
    barrier = pltpu.get_barrier_semaphore()
    for device in ((r, core), (r, chip), (beside, c)):
        pl.semaphore_signal(barrier, inc=1, device_id=device, device_id_type=MESH)

    @pl.when(has_up)
    def _():
        pl.semaphore_signal(barrier, inc=1, device_id=(up, c), device_id_type=MESH)

    @pl.when(has_down)
    def _():
        pl.semaphore_signal(barrier, inc=1, device_id=(down, c), device_id_type=MESH)

    pl.semaphore_wait(barrier, 3 + has_up.astype(jnp.int32) + has_down.astype(jnp.int32))
    load.wait()

    def columns(p, offset=0):
        start = offset + p * step
        return pl.ds(start if isinstance(start, int) else pl.multiple_of(start, 128), step)

    def send(src, dst, q, p, send_sem, recv_sem, device):
        return pltpu.make_async_remote_copy(
            src_ref=src.at[q, :, columns(p)], dst_ref=dst.at[q, :, columns(p)], send_sem=send_sem, recv_sem=recv_sem,
            device_id=device, device_id_type=MESH,
        )

    def row_copy(t, p):
        device = (r, chip) if t == 2 else (r, core)
        return send(rows, rows, chip if t == 3 else c, p, row_send.at[t - 1, p], row_recv.at[t - 1, p], device)

    def up_copy(src, t, p):
        return send(src, own, order[t], p, up_send.at[t, p], own_recv.at[t, p], (up, c))

    def down_copy(src, t, p):
        return send(src, own, order[t], p, down_send.at[t, p], own_recv.at[t, p], (down, c))

    def swap_copy(src, t, p):
        return send(src, other, order[t], p, swap_send.at[t, p], swap_recv.at[t, p], (beside, c))

    def alt_up_copy(src, t, p):
        return send(src, alt, alt_order[t], p, alt_up_send.at[t - 2, p], alt_recv.at[t - 2, p], (up, c))

    def alt_down_copy(src, t, p):
        return send(src, alt, alt_order[t], p, alt_down_send.at[t - 2, p], alt_recv.at[t - 2, p], (down, c))

    def cross_copy(src, t, p):
        return send(src, own, alt_order[t], p, cross_send.at[t - 2, p], own_recv.at[t, p], (r, chip))

    def put_rhs(src, q, p, offset):
        hi, lo = split(src[q, :, columns(p)])
        at = columns(p, offset)
        first = pl.multiple_of(q * depth, depth)
        rhs_ref[pl.ds(first, depth), at] = hi
        rhs_ref[pl.ds(pl.multiple_of(pairs + q * depth, depth), depth), at] = lo

    def finish(src, t, p):
        if p < SWAPPED:
            swap_copy(src, t, p).start()
        else:
            first = pl.multiple_of(order[t] * depth, depth)
            tail_ref[pl.ds(first, depth), columns(p - SWAPPED)] = src[order[t], :, columns(p)]
        put_rhs(src, order[t], p, place * width)

    for p in range(PIECES):
        row_copy(2, p).start()
        row_copy(1, p).start()

    def away(p):
        return ALTERNATE[p % len(ALTERNATE)]

    def originate(p):
        for t in range(groups):
            if t > 0:
                row_copy(t, p).wait_recv()
            if t == 2:
                row_copy(3, p).start()

            @pl.when(source)
            def _():
                if t not in away(p):
                    @pl.when(has_up)
                    def _():
                        up_copy(rows, t, p).start()

                    @pl.when(has_down)
                    def _():
                        down_copy(rows, t, p).start()

                finish(rows, t, p)

            for s in away(p) if t == 1 else ():
                @pl.when(alt_source)
                def _():
                    @pl.when(has_up)
                    def _():
                        alt_up_copy(rows, s, p).start()

                    @pl.when(has_down)
                    def _():
                        alt_down_copy(rows, s, p).start()

    def relay(p):
        for t in range(groups):
            if t not in away(p):
                @pl.when(jnp.logical_not(source))
                def _():
                    up_copy(own, t, p).wait_recv()

                    @pl.when(send_up)
                    def _():
                        up_copy(own, t, p).start()

                    @pl.when(send_down)
                    def _():
                        down_copy(own, t, p).start()

                    finish(own, t, p)

        for t in away(p):
            @pl.when(jnp.logical_not(alt_source))
            def _():
                alt_up_copy(alt, t, p).wait_recv()

                @pl.when(alt_send_up)
                def _():
                    alt_up_copy(alt, t, p).start()

                @pl.when(alt_send_down)
                def _():
                    alt_down_copy(alt, t, p).start()

                cross_copy(alt, t, p).start()

    def crossed(p):
        for t in away(p):
            @pl.when(jnp.logical_not(source))
            def _():
                up_copy(own, t, p).wait_recv()
                finish(own, t, p)

    def put_lhs(p):
        block = rows[:, :, columns(p)].reshape(pairs, step).T
        for f in range(w_ref.shape[0]):
            hi, lo = split(block * w_ref[f:f + 1, :])
            lhs_ref[f, columns(p), 0:pairs] = hi
            lhs_ref[f, columns(p), pairs:2 * pairs] = lo

    for turn in range(PIECES + LEAD + CROSS_LAG):
        if turn < PIECES:
            originate(turn)
        if 0 <= turn - LEAD < PIECES:
            relay(turn - LEAD)
        if 0 <= turn - LEAD - CROSS_LAG < PIECES:
            crossed(turn - LEAD - CROSS_LAG)
        if 0 <= turn - LEAD < PIECES:
            put_lhs(turn - LEAD)

    for p in range(SWAPPED):
        for t in range(groups):
            swap_copy(own, t, p).wait_recv()
            put_rhs(other, order[t], p, (1 - place) * width)
    for p in range(PIECES):
        for t in range(groups):
            if t > 0:
                row_copy(t, p).wait_send()
            if p < SWAPPED:
                swap_copy(own, t, p).wait_send()
            if t in away(p):
                @pl.when(alt_send_up)
                def _():
                    alt_up_copy(alt, t, p).wait_send()

                @pl.when(alt_send_down)
                def _():
                    alt_down_copy(alt, t, p).wait_send()

                @pl.when(jnp.logical_not(alt_source))
                def _():
                    cross_copy(alt, t, p).wait_send()
            else:
                @pl.when(send_up)
                def _():
                    up_copy(own, t, p).wait_send()

                @pl.when(send_down)
                def _():
                    down_copy(own, t, p).wait_send()


def gather(mel, weights, span):
    depth, width = mel.shape
    nf = weights.shape[0]
    dma = pltpu.SemaphoreType.DMA
    four, two = dma((4, PIECES)), dma((2, PIECES))
    vmem = pl.BlockSpec(memory_space=pltpu.VMEM)
    return pl.pallas_call(
        functools.partial(gather_kernel, span),
        out_shape=(
            jax.ShapeDtypeStruct((nf, width, 8 * depth), jnp.bfloat16),
            jax.ShapeDtypeStruct((8 * depth, span * width), jnp.bfloat16),
            jax.ShapeDtypeStruct((4 * depth, width - SWAPPED * (width // PIECES)), jnp.float32),
        ),
        in_specs=[vmem, pl.BlockSpec(memory_space=pl.ANY)],
        out_specs=(vmem, vmem, vmem),
        scratch_shapes=[pltpu.VMEM((4, depth, width), jnp.float32)] * 4
        + [dma, dma((3, PIECES)), dma((3, PIECES))]
        + [four] * 5 + [two] * 4,
        compiler_params=pltpu.CompilerParams(
            collective_id=0, has_side_effects=True, vmem_limit_bytes=20 * MIB
        ),
    )(weights, mel)


def multiply(lhs_ref, rhs_hi, rhs_lo, out_ref):
    height = out_ref.shape[1]
    pairs = rhs_hi.shape[0]
    at = pl.ds(pl.multiple_of(pl.program_id(1) * height, height), height)
    right = jnp.concatenate([rhs_hi, rhs_hi, rhs_lo], axis=0)
    for f in range(out_ref.shape[0]):
        left = lhs_ref[f, at, :]
        out_ref[f] = jnp.dot(
            jnp.concatenate([left, left[:, :pairs]], axis=1), right, preferred_element_type=jnp.float32
        )


def first_kernel(place_ref, lhs_ref, rhs_ref, out_ref):
    pairs = rhs_ref.shape[0] // 2
    tile = out_ref.shape[2]
    count = rhs_ref.shape[1] // tile
    index = (pl.program_id(0) + place_ref[0] * (count // 2)) % count
    at = pl.ds(pl.multiple_of(index * tile, tile), tile)
    multiply(lhs_ref, rhs_ref[:pairs, at], rhs_ref[pairs:, at], out_ref)


def second_kernel(place_ref, lhs_ref, tail_ref, rhs_ref, done_ref, out_ref):
    tile = out_ref.shape[2]
    at = pl.ds(pl.multiple_of(pl.program_id(0) * tile, tile), tile)
    hi, lo = split(tail_ref[:, at])
    multiply(lhs_ref, hi, lo, out_ref)


def product(lhs, rhs, tail, place, tail_of):
    nf, width, _ = lhs.shape
    columns = rhs.shape[1]
    tile = width // 3
    height = width // 2
    count = columns // tile
    last = tail.shape[1] // tile
    out = jax.ShapeDtypeStruct((nf, width, columns), jnp.float32)
    vmem = pl.BlockSpec(memory_space=pltpu.VMEM)

    def call(kernel, start, steps, operands, specs, aliases):
        flops = 2 * 3 * nf * width * PAIRS * tile * steps
        return pl.pallas_call(
            kernel,
            out_shape=out,
            grid_spec=pltpu.PrefetchScalarGridSpec(
                num_scalar_prefetch=1,
                grid=(steps, width // height),
                in_specs=specs,
                out_specs=pl.BlockSpec(
                    (nf, height, tile), lambda i, m, at: (0, m, (i + start + at[0] * (count // 2)) % count)
                ),
            ),
            input_output_aliases=aliases,
            cost_estimate=pl.CostEstimate(
                flops=flops, bytes_accessed=nf * width * tile * steps * 4, transcendentals=0
            ),
            compiler_params=pltpu.CompilerParams(vmem_limit_bytes=32 * MIB),
        )(place, *operands)

    done = call(first_kernel, 0, count - last, (lhs, rhs), [vmem, vmem], {})
    return call(
        second_kernel, count - last, last, (lhs, tail_of(tail), rhs, done),
        [vmem] * 3 + [pl.BlockSpec(memory_space=pl.ANY)], {4: 0},
    )


def body(rows, cols, mel, pair_val, pair_cond, val_energy, cond_energy, freqs):
    weights = pair_weights(pair_val, pair_cond, val_energy, cond_energy, freqs)
    if cols == 4 and rows == 8 and mel.shape[0] % 16 == 0 and mel.shape[1] % (128 * PIECES) == 0:
        span = rows // cols
        place = (lax.axis_index("row") % span).astype(jnp.int32)[None]
        pairs = [(r, r + 1 - 2 * (r % span)) for r in range(rows)]
        return product(*gather(mel, weights, span), place, lambda tail: lax.ppermute(tail, "row", pairs))
    rows_all = lax.all_gather(mel, "col", axis=0, tiled=True)
    own_block = lax.all_gather(mel, "row", axis=1, tiled=True)
    col_block = lax.all_to_all(own_block, "col", split_axis=1, concat_axis=0, tiled=True)
    scaled = weights[:, :, None] * rows_all[None, :, :]
    return lax.dot_general(
        scaled,
        col_block,
        (((1,), (0,)), ((), ())),
        precision=lax.Precision.HIGHEST,
        preferred_element_type=jnp.float32,
    )


def solution(mesh):
    return jax.shard_map(
        functools.partial(body, mesh.shape["row"], mesh.shape["col"]),
        mesh=mesh,
        in_specs=(P("col", "row"), P(), P(), P(), P(), P()),
        out_specs=P(None, "row", "col"),
        check_vma=False,
    )
```

```python
import functools
import math

import jax
import jax.numpy as jnp
from jax import lax
from jax.experimental import pallas as pl
from jax.experimental.pallas import tpu as pltpu
from jax.sharding import PartitionSpec as P

PAIRS = 128
MESH = pl.DeviceIdType.MESH
PIECES = 3
SWAPPED = 1
LEAD = 3
CROSS_LAG = 1
ALTERNATE = ((3,), (2, 3))
MIB = 1024 * 1024


def pair_weights(pair_val, pair_cond, val_energy, cond_energy, freqs):
    cond_onehot = (
        pair_cond[:, None] == jnp.arange(cond_energy.shape[0], dtype=jnp.int32)[None, :]
    ).astype(jnp.float32)
    val_onehot = (
        pair_val[:, None] == jnp.arange(val_energy.shape[0], dtype=jnp.int32)[None, :]
    ).astype(jnp.float32)
    gap = jnp.sum(cond_onehot * cond_energy[None, :], axis=1) - jnp.sum(
        val_onehot * val_energy[None, :], axis=1
    )
    scale = 1.0 / math.sqrt(PAIRS)
    return (
        -4.0
        * gap[None, :]
        / (gap[None, :] * gap[None, :] + freqs[:, None] * freqs[:, None])
        * scale
    )


def split(x):
    hi = x.astype(jnp.bfloat16)
    return hi, (x - hi.astype(jnp.float32)).astype(jnp.bfloat16)


def gather_kernel(
    span, w_ref, mel_ref, lhs_ref, rhs_ref, tail_ref, rows, own, other, alt,
    load_sem, row_send, row_recv, up_send, down_send, own_recv, swap_send, swap_recv,
    alt_up_send, alt_down_send, alt_recv, cross_send,
):
    r, c = lax.axis_index("row"), lax.axis_index("col")
    group, place = r // span, r % span
    depth, width = mel_ref.shape
    groups = 4
    pairs = groups * depth
    step = width // PIECES
    core = c + 1 - 2 * (c % 2)
    chip = c + 2 - 4 * (c // 2)
    both = core + 2 - 4 * (core // 2)
    order = (c, core, chip, both)
    alt_order = (chip, both, c, core)
    beside = r + 1 - 2 * place
    up, down = r + span, r - span
    has_up, has_down = group < groups - 1, group > 0
    source, alt_source = group == c, group == chip
    send_up, send_down = (group >= c) & has_up, (group <= c) & has_down
    alt_send_up, alt_send_down = (group >= chip) & has_up, (group <= chip) & has_down

    load = pltpu.make_async_copy(mel_ref, rows.at[c], load_sem)
    load.start()
    barrier = pltpu.get_barrier_semaphore()
    for device in ((r, core), (r, chip), (beside, c)):
        pl.semaphore_signal(barrier, inc=1, device_id=device, device_id_type=MESH)

    @pl.when(has_up)
    def _():
        pl.semaphore_signal(barrier, inc=1, device_id=(up, c), device_id_type=MESH)

    @pl.when(has_down)
    def _():
        pl.semaphore_signal(barrier, inc=1, device_id=(down, c), device_id_type=MESH)

    pl.semaphore_wait(barrier, 3 + has_up.astype(jnp.int32) + has_down.astype(jnp.int32))
    load.wait()

    def columns(p, offset=0):
        start = offset + p * step
        return pl.ds(start if isinstance(start, int) else pl.multiple_of(start, 128), step)

    def send(src, dst, q, p, send_sem, recv_sem, device):
        return pltpu.make_async_remote_copy(
            src_ref=src.at[q, :, columns(p)], dst_ref=dst.at[q, :, columns(p)], send_sem=send_sem, recv_sem=recv_sem,
            device_id=device, device_id_type=MESH,
        )

    def row_copy(t, p):
        device = (r, chip) if t == 2 else (r, core)
        return send(rows, rows, chip if t == 3 else c, p, row_send.at[t - 1, p], row_recv.at[t - 1, p], device)

    def up_copy(src, t, p):
        return send(src, own, order[t], p, up_send.at[t, p], own_recv.at[t, p], (up, c))

    def down_copy(src, t, p):
        return send(src, own, order[t], p, down_send.at[t, p], own_recv.at[t, p], (down, c))

    def swap_copy(src, t, p):
        return send(src, other, order[t], p, swap_send.at[t, p], swap_recv.at[t, p], (beside, c))

    def alt_up_copy(src, t, p):
        return send(src, alt, alt_order[t], p, alt_up_send.at[t - 2, p], alt_recv.at[t - 2, p], (up, c))

    def alt_down_copy(src, t, p):
        return send(src, alt, alt_order[t], p, alt_down_send.at[t - 2, p], alt_recv.at[t - 2, p], (down, c))

    def cross_copy(src, t, p):
        return send(src, own, alt_order[t], p, cross_send.at[t - 2, p], own_recv.at[t, p], (r, chip))

    def put_rhs(src, q, p, offset):
        hi, lo = split(src[q, :, columns(p)])
        at = columns(p, offset)
        first = pl.multiple_of(q * depth, depth)
        rhs_ref[pl.ds(first, depth), at] = hi
        rhs_ref[pl.ds(pl.multiple_of(pairs + q * depth, depth), depth), at] = lo

    def finish(src, t, p):
        if p < SWAPPED:
            swap_copy(src, t, p).start()
        else:
            first = pl.multiple_of(order[t] * depth, depth)
            tail_ref[pl.ds(first, depth), columns(p - SWAPPED)] = src[order[t], :, columns(p)]
        put_rhs(src, order[t], p, place * width)

    for p in range(PIECES):
        row_copy(2, p).start()
        row_copy(1, p).start()

    def away(p):
        return ALTERNATE[p % len(ALTERNATE)]

    def originate(p):
        for t in range(groups):
            if t > 0:
                row_copy(t, p).wait_recv()
            if t == 2:
                row_copy(3, p).start()

            @pl.when(source)
            def _():
                if t not in away(p):
                    @pl.when(has_up)
                    def _():
                        up_copy(rows, t, p).start()

                    @pl.when(has_down)
                    def _():
                        down_copy(rows, t, p).start()

                finish(rows, t, p)

            for s in away(p) if t == 1 else ():
                @pl.when(alt_source)
                def _():
                    @pl.when(has_up)
                    def _():
                        alt_up_copy(rows, s, p).start()

                    @pl.when(has_down)
                    def _():
                        alt_down_copy(rows, s, p).start()

    def relay(p):
        for t in range(groups):
            if t not in away(p):
                @pl.when(jnp.logical_not(source))
                def _():
                    up_copy(own, t, p).wait_recv()

                    @pl.when(send_up)
                    def _():
                        up_copy(own, t, p).start()

                    @pl.when(send_down)
                    def _():
                        down_copy(own, t, p).start()

                    finish(own, t, p)

        for t in away(p):
            @pl.when(jnp.logical_not(alt_source))
            def _():
                alt_up_copy(alt, t, p).wait_recv()

                @pl.when(alt_send_up)
                def _():
                    alt_up_copy(alt, t, p).start()

                @pl.when(alt_send_down)
                def _():
                    alt_down_copy(alt, t, p).start()

                cross_copy(alt, t, p).start()

    def crossed(p):
        for t in away(p):
            @pl.when(jnp.logical_not(source))
            def _():
                up_copy(own, t, p).wait_recv()
                finish(own, t, p)

    def put_lhs(p):
        block = rows[:, :, columns(p)].reshape(pairs, step).T
        for f in range(w_ref.shape[0]):
            hi, lo = split(block * w_ref[f:f + 1, :])
            lhs_ref[f, columns(p), 0:pairs] = hi
            lhs_ref[f, columns(p), pairs:2 * pairs] = lo

    for turn in range(PIECES + LEAD + CROSS_LAG):
        if turn < PIECES:
            originate(turn)
        if 0 <= turn - LEAD < PIECES:
            relay(turn - LEAD)
        if 0 <= turn - LEAD - CROSS_LAG < PIECES:
            crossed(turn - LEAD - CROSS_LAG)
        if 0 <= turn - LEAD < PIECES:
            put_lhs(turn - LEAD)

    for p in range(SWAPPED):
        for t in range(groups):
            swap_copy(own, t, p).wait_recv()
            put_rhs(other, order[t], p, (1 - place) * width)
    for p in range(PIECES):
        for t in range(groups):
            if t > 0:
                row_copy(t, p).wait_send()
            if p < SWAPPED:
                swap_copy(own, t, p).wait_send()
            if t in away(p):
                @pl.when(alt_send_up)
                def _():
                    alt_up_copy(alt, t, p).wait_send()

                @pl.when(alt_send_down)
                def _():
                    alt_down_copy(alt, t, p).wait_send()

                @pl.when(jnp.logical_not(alt_source))
                def _():
                    cross_copy(alt, t, p).wait_send()
            else:
                @pl.when(send_up)
                def _():
                    up_copy(own, t, p).wait_send()

                @pl.when(send_down)
                def _():
                    down_copy(own, t, p).wait_send()


def gather(mel, weights, span):
    depth, width = mel.shape
    nf = weights.shape[0]
    dma = pltpu.SemaphoreType.DMA
    four, two = dma((4, PIECES)), dma((2, PIECES))
    vmem = pl.BlockSpec(memory_space=pltpu.VMEM)
    return pl.pallas_call(
        functools.partial(gather_kernel, span),
        out_shape=(
            jax.ShapeDtypeStruct((nf, width, 8 * depth), jnp.bfloat16),
            jax.ShapeDtypeStruct((8 * depth, span * width), jnp.bfloat16),
            jax.ShapeDtypeStruct((4 * depth, width - SWAPPED * (width // PIECES)), jnp.float32),
        ),
        in_specs=[vmem, pl.BlockSpec(memory_space=pl.ANY)],
        out_specs=(vmem, vmem, vmem),
        scratch_shapes=[pltpu.VMEM((4, depth, width), jnp.float32)] * 4
        + [dma, dma((3, PIECES)), dma((3, PIECES))]
        + [four] * 5 + [two] * 4,
        compiler_params=pltpu.CompilerParams(
            collective_id=0, has_side_effects=True, vmem_limit_bytes=20 * MIB
        ),
    )(weights, mel)


def multiply(lhs_ref, rhs_hi, rhs_lo, out_ref):
    height = out_ref.shape[1]
    pairs = rhs_hi.shape[0]
    at = pl.ds(pl.multiple_of(pl.program_id(1) * height, height), height)
    right = jnp.concatenate([rhs_hi, rhs_hi, rhs_lo], axis=0)
    for f in range(out_ref.shape[0]):
        left = lhs_ref[f, at, :]
        out_ref[f] = jnp.dot(
            jnp.concatenate([left, left[:, :pairs]], axis=1), right, preferred_element_type=jnp.float32
        )


def first_kernel(place_ref, lhs_ref, rhs_ref, out_ref):
    pairs = rhs_ref.shape[0] // 2
    tile = out_ref.shape[2]
    count = rhs_ref.shape[1] // tile
    index = (pl.program_id(0) + place_ref[0] * (count // 2)) % count
    at = pl.ds(pl.multiple_of(index * tile, tile), tile)
    multiply(lhs_ref, rhs_ref[:pairs, at], rhs_ref[pairs:, at], out_ref)


def second_kernel(place_ref, lhs_ref, tail_ref, rhs_ref, done_ref, out_ref):
    tile = out_ref.shape[2]
    at = pl.ds(pl.multiple_of(pl.program_id(0) * tile, tile), tile)
    hi, lo = split(tail_ref[:, at])
    multiply(lhs_ref, hi, lo, out_ref)


def product(lhs, rhs, tail, place, tail_of):
    nf, width, _ = lhs.shape
    columns = rhs.shape[1]
    tile = width // 3
    height = width // 2
    count = columns // tile
    last = tail.shape[1] // tile
    out = jax.ShapeDtypeStruct((nf, width, columns), jnp.float32)
    vmem = pl.BlockSpec(memory_space=pltpu.VMEM)

    def call(kernel, start, steps, operands, specs, aliases):
        flops = 2 * 3 * nf * width * PAIRS * tile * steps
        return pl.pallas_call(
            kernel,
            out_shape=out,
            grid_spec=pltpu.PrefetchScalarGridSpec(
                num_scalar_prefetch=1,
                grid=(steps, width // height),
                in_specs=specs,
                out_specs=pl.BlockSpec(
                    (nf, height, tile), lambda i, m, at: (0, m, (i + start + at[0] * (count // 2)) % count)
                ),
            ),
            input_output_aliases=aliases,
            cost_estimate=pl.CostEstimate(
                flops=flops, bytes_accessed=nf * width * tile * steps * 4, transcendentals=0
            ),
            compiler_params=pltpu.CompilerParams(vmem_limit_bytes=32 * MIB),
        )(place, *operands)

    done = call(first_kernel, 0, count - last, (lhs, rhs), [vmem, vmem], {})
    return call(
        second_kernel, count - last, last, (lhs, tail_of(tail), rhs, done),
        [vmem] * 3 + [pl.BlockSpec(memory_space=pl.ANY)], {4: 0},
    )


def body(rows, cols, mel, pair_val, pair_cond, val_energy, cond_energy, freqs):
    weights = pair_weights(pair_val, pair_cond, val_energy, cond_energy, freqs)
    if cols == 4 and rows == 8 and mel.shape[0] % 16 == 0 and mel.shape[1] % (128 * PIECES) == 0:
        span = rows // cols
        place = (lax.axis_index("row") % span).astype(jnp.int32)[None]
        pairs = [(r, r + 1 - 2 * (r % span)) for r in range(rows)]
        return product(*gather(mel, weights, span), place, lambda tail: lax.ppermute(tail, "row", pairs))
    rows_all = lax.all_gather(mel, "col", axis=0, tiled=True)
    own_block = lax.all_gather(mel, "row", axis=1, tiled=True)
    col_block = lax.all_to_all(own_block, "col", split_axis=1, concat_axis=0, tiled=True)
    scaled = weights[:, :, None] * rows_all[None, :, :]
    return lax.dot_general(
        scaled,
        col_block,
        (((1,), (0,)), ((), ())),
        precision=lax.Precision.HIGHEST,
        preferred_element_type=jnp.float32,
    )


def solution(mesh):
    return jax.shard_map(
        functools.partial(body, mesh.shape["row"], mesh.shape["col"]),
        mesh=mesh,
        in_specs=(P("col", "row"), P(), P(), P(), P(), P()),
        out_specs=P(None, "row", "col"),
        check_vma=False,
    )
```
